32 devices in a mesh: grp: 8 (over y, x, core), col: 4 (over z).
Axes of the slice: x: 2, y: 2, z: 4, core: 2. Of those that a mesh axis runs over, the one named last changes fastest.
Arguments:
- states: bfloat16 [16, 32768], P(None, ('grp', 'col')), may hold values from -6 to 6
- gaps: float32 [16, 32768], P(None, ('grp', 'col')), may hold values from 1 to 4
- tiles: bfloat16 [8192, 128, 128], P(('grp', 'col')), may hold values from -0.09375 to 0.09375
- tile_index: int32 [8192], P(('grp', 'col')), may hold values from -1 to 1535, as said below
- xor_masks: int32 [5], replicated, may hold values from 1 to 7, as said below
- ritz_level: int32 [16], replicated, may hold values from 0 to 15
Outputs:
- corrected: float32 [16, 32768], P(None, ('grp', 'col'))
The draws below stay inside these ranges and needn't reach their ends.
Inputs may be any that keep to these rules, and one draw needn't show every extreme that they name: Matching j pairs group g with group g XOR xor_masks[j]; in every draw the masks include half the number of groups, the number of groups minus one, and 1. `tile_index`: the codes of one device's live slots are distinct; its live slots come first and empty ones (-1) last; some device has all 256 slots live in every draw.
All inputs are finite; a program needn't handle non-finite values.
Results may differ from the reference program's by a relative error of at most 0.0027.
Values may be sent and summed in bfloat16 or wider, within the bound.
No kernel may reach another device: no remote copies, remote signals or barrier semaphores. Data moves between devices by JAX's collectives and lax.ppermute only.
A program may use at most 64 MiB of HBM per device.

```python
import math
import jax
import jax.numpy as jnp
from jax import lax

STATES = 16
TILE = 128
GROUP_ROWS = 4096
MATCHINGS = 5
SWEEPS = 2
SLOTS = 256
COUPLINGS = 6
ROWS = 32768
TILE_ROWS = 32
TILE_COLS = 8
TOTAL_SLOTS = 8192
N_GRP = 8
N_COL = 4


def draw_tile_index(key, part):
    positions = COUPLINGS * TILE_ROWS * TILE_COLS
    devices = N_GRP * N_COL
    device_keys = jax.random.split(jax.random.fold_in(key, 11), devices)

    def choose_positions(device_key):
        return jax.random.permutation(device_key, positions)[:SLOTS].astype(jnp.int32)
    picks = jax.vmap(choose_positions)(device_keys)
    levels = jax.random.randint(jax.random.fold_in(key, 12), (devices,), 1, 9)
    busiest = jax.random.randint(jax.random.fold_in(key, 13), (), 0, devices)
    levels = jnp.where(jnp.arange(devices) == busiest, 8, levels)
    counts = jnp.maximum(SLOTS * levels * levels // 64, 1)
    live_slot = jnp.arange(SLOTS)[None, :] < counts[:, None]
    return jnp.where(live_slot, picks, -1).reshape(-1).astype(jnp.int32)


def draw_xor_masks(key, part):
    masks = jax.random.randint(jax.random.fold_in(key, 21), (MATCHINGS,), 1, N_GRP)
    order = jax.random.permutation(jax.random.fold_in(key, 22), MATCHINGS)
    masks = jnp.where(order == 0, N_GRP // 2, masks)
    masks = jnp.where(order == 1, N_GRP - 1, masks)
    masks = jnp.where(order == 2, 1, masks)
    return masks.astype(jnp.int32)


def place_ends(entries, key, smallest, top_value):
    longest = entries.shape.index(max(entries.shape))
    spots = []
    for shift in (0, 1):
        where = [jax.random.randint(jax.random.fold_in(key, axis), (), 0, length) for axis, length in enumerate(entries.shape)]
        where[longest] = (where[longest] + shift) % entries.shape[longest]
        spots.append(tuple(where))
    return entries.at[spots[0]].set(smallest).at[spots[1]].set(top_value)


def block_scale(own_key, shape, pieces, smallest, high):
    loudness = 1.0
    for axis_at, parts in pieces:
        steps = jax.random.uniform(jax.random.fold_in(jax.random.fold_in(own_key, 6), axis_at), (parts,), jnp.float32, smallest / len(pieces), high / len(pieces))
        loudness = loudness * jnp.repeat(jnp.exp(steps), shape[axis_at] // parts).reshape((-1,) + (1,) * (len(shape) - 1 - axis_at))
    return loudness


def noise(key, extent, scale, reach, cuts=(), kind=jnp.bfloat16):
    drawn = scale * jax.random.normal(key, extent, jnp.float32)
    if cuts:
        drawn = drawn * block_scale(key, extent, cuts, -0.22, 0.18)
    return jnp.clip(drawn, -reach, reach).astype(kind)


def setup_inputs(seed: int = 0) -> dict:
    seeds = jax.random.split(jax.random.key(seed), 7)
    states = noise(seeds[0], (STATES, ROWS), 1.0, 6.0, ((1, 32),))
    gaps = jnp.clip(jnp.exp(math.log(4.0) - 1.3862944 * jax.random.uniform(seeds[1], (STATES, ROWS), jnp.float32) ** block_scale(seeds[1], (STATES, ROWS), ((1, 32),), -0.2, 0.2)), 1.0, 4.0)
    tiles = noise(seeds[2], (TOTAL_SLOTS, TILE, TILE), (SLOTS * N_COL * TILE // TILE_ROWS) ** -0.5, 0.09375, ((0, 32),))
    tile_index = draw_tile_index(jax.random.fold_in(seeds[6], 71), 0)
    xor_masks = draw_xor_masks(jax.random.fold_in(seeds[6], 71), 0)
    ritz_level = place_ends(jax.random.randint(seeds[5], (STATES,), 0, 16), jax.random.fold_in(seeds[5], 1), 0, 15).astype(jnp.int32)
    return {"states": states, "gaps": gaps, "tiles": tiles, "tile_index": tile_index, "xor_masks": xor_masks, "ritz_level": ritz_level}


def reference(states, gaps, tiles, tile_index, xor_masks, ritz_level):
    tile_cols = GROUP_ROWS // (TILE * N_COL)
    tile_rows = GROUP_ROWS // TILE
    tile_groups = tiles.reshape(N_GRP, N_COL, SLOTS, TILE, TILE)
    slot_codes = tile_index.reshape(N_GRP, N_COL, SLOTS)
    shifts = ritz_level.astype(jnp.float32) * 0.125 - 1.0
    group_ids = jnp.arange(N_GRP, dtype=jnp.int32)
    partner_ids = jnp.stack([group_ids] + [jnp.bitwise_xor(group_ids, xor_masks[match_id]) for match_id in range(MATCHINGS)], axis=1)

    def apply_matrix(current):
        grouped = current.reshape(STATES, N_GRP, N_COL, tile_cols, TILE)

        def one_group(group_id):
            sources = jnp.take(grouped, partner_ids[group_id], axis=1)
            sources = jnp.transpose(sources, (2, 1, 3, 0, 4)).reshape(N_COL, COUPLINGS * tile_cols, STATES, TILE)
            codes_here = slot_codes[group_id]
            live_slot = codes_here >= 0
            safe_code = jnp.maximum(codes_here, 0)
            coupling = safe_code // (tile_rows * tile_cols)
            tile_row = (safe_code // tile_cols) % tile_rows
            tile_col = safe_code % tile_cols
            source_id = (coupling * tile_cols + tile_col).astype(jnp.int32)
            picked = jnp.take_along_axis(sources, source_id[:, :, None, None], axis=1)
            products = jnp.einsum('csqb,csrb->csqr', picked.astype(jnp.float32), tile_groups[group_id].astype(jnp.float32))
            products = products * live_slot[:, :, None, None].astype(jnp.float32)
            placement = ((tile_row[:, :, None] == jnp.arange(tile_rows, dtype=jnp.int32)[None, None, :]) & live_slot[:, :, None]).astype(jnp.float32)
            summed = jnp.einsum('cst,csqr->qtr', placement, products, precision=lax.Precision.HIGHEST)
            return summed.reshape(STATES, GROUP_ROWS)

        results = lax.map(one_group, group_ids)
        return jnp.transpose(results, (1, 0, 2)).reshape(STATES, N_GRP * GROUP_ROWS)

    current = states
    updated = states.astype(jnp.float32)
    for sweep_number in range(SWEEPS):
        product_sum = apply_matrix(current)
        previous = current.astype(jnp.float32)
        residual = product_sum - shifts[:, None] * previous
        updated = previous - residual / gaps
        if sweep_number + 1 < SWEEPS:
            current = updated.astype(jnp.bfloat16)
    return updated
```

```python
import functools
import math
import jax
import jax.numpy as jnp
from jax import lax
from jax.experimental import pallas as pl
from jax.experimental.pallas import tpu as pltpu
from jax.sharding import PartitionSpec as P

SWEEPS = 2


def xor_pairs(size, mask):
    return [(i, i ^ mask) for i in range(size)]


def product_kernel(quarters, unroll, where_ref, *refs):
    source_ref, tiles_ref = refs[0], refs[1]
    outs, acc = refs[2 : 2 + quarters], refs[2 + quarters]
    slots, tile_size = tiles_ref.shape[0], tiles_ref.shape[1]
    states = source_ref.shape[1]
    acc[...] = jnp.zeros_like(acc)

    @pl.loop(0, slots // unroll)
    def _(step):
        products = []
        for pair in range(0, unroll, 2):
            slot = step * unroll + pair
            picked = jnp.concatenate([source_ref[where_ref[0, slot + i]] for i in range(2)], axis=0)
            two = tiles_ref[pl.ds(slot, 2)].reshape(2 * tile_size, tile_size)
            product = lax.dot_general(picked, two, (((1,), (1,)), ((), ())), preferred_element_type=jnp.float32)
            products += [product[:states, :tile_size], product[states:, tile_size:]]
        for i in range(unroll):
            acc[where_ref[1, step * unroll + i]] += products[i]

    rows = outs[0].shape[0]
    for i, out in enumerate(outs):
        out[...] = acc[i * rows : (i + 1) * rows].astype(out.dtype)


def tile_products(where, source, tiles, quarters, rows):
    slots, tile_size = tiles.shape[0], tiles.shape[1]
    states = source.shape[1]
    block = (rows, states, tile_size)
    vmem = pl.BlockSpec(memory_space=pltpu.VMEM)
    return pl.pallas_call(
        functools.partial(product_kernel, quarters, math.gcd(slots, 64)),
        out_shape=[jax.ShapeDtypeStruct(block, jnp.float32 if i == 0 else jnp.bfloat16) for i in range(quarters)],
        in_specs=[pl.BlockSpec(memory_space=pltpu.SMEM), vmem, vmem],
        out_specs=[vmem] * quarters,
        scratch_shapes=[pltpu.VMEM((quarters * rows + 1, states, tile_size), jnp.float32)],
        compiler_params=pltpu.CompilerParams(vmem_limit_bytes=16 << 20),
        cost_estimate=pl.CostEstimate(
            flops=2 * slots * states * tile_size * tile_size, bytes_accessed=0, transcendentals=0
        ),
        name="tile_products",
    )(where, source, tiles)


def per_device(states, gaps, tiles, tile_index, xor_masks, ritz_level):
    groups, quarters = lax.axis_size("grp"), lax.axis_size("col")
    state_count, row_slice = states.shape
    tile_size = tiles.shape[1]
    tile_cols = row_slice // tile_size
    tile_rows = tile_cols * quarters

    def blocked(a):
        return jnp.transpose(a.reshape(state_count, tile_cols, tile_size), (1, 0, 2))

    my_col = lax.axis_index("col")
    live = tile_index >= 0
    code = jnp.maximum(tile_index, 0)
    coupling = code // (tile_rows * tile_cols)
    row = code // tile_cols % tile_rows
    mask = jnp.zeros_like(code)
    for i in range(xor_masks.shape[0]):
        mask = jnp.where(coupling == i + 1, xor_masks[i], mask)
    place = mask // 2 + mask % 2 * (groups // 2)
    source_id = jnp.where(live, place * tile_cols + code % tile_cols, 0)
    row_id = jnp.bitwise_xor(row // tile_cols, my_col) * tile_cols + row % tile_cols
    row_id = jnp.where(live, row_id, tile_rows)
    where = jnp.stack([source_id, row_id]).astype(jnp.int32)

    shifts = (ritz_level.astype(jnp.float32) * 0.125 - 1.0)[None, :, None]
    gaps = blocked(gaps)
    current = blocked(states)
    for sweep in range(SWEEPS):
        near = [current] + [lax.ppermute(current, "grp", xor_pairs(groups, k)) for k in range(2, groups, 2)]
        near = jnp.concatenate(near, axis=0)
        far = lax.ppermute(near, "grp", xor_pairs(groups, 1))
        source = jnp.concatenate([near, far], axis=0)
        sums = tile_products(where, source, tiles, quarters, tile_cols)
        product_sum = sums[0]
        for k in range(1, quarters):
            product_sum = product_sum + lax.ppermute(sums[k], "col", xor_pairs(quarters, k)).astype(jnp.float32)
        previous = current.astype(jnp.float32)
        updated = previous - (product_sum - shifts * previous) / gaps
        current = updated.astype(jnp.bfloat16)
    return jnp.transpose(updated, (1, 0, 2)).reshape(state_count, row_slice)


def solution(mesh):
    placed = (
        P(None, ("grp", "col")),
        P(None, ("grp", "col")),
        P(("grp", "col"), None, None),
        P(("grp", "col")),
        P(),
        P(),
    )
    return jax.shard_map(
        per_device, mesh=mesh, in_specs=placed, out_specs=P(None, ("grp", "col")), check_vma=False
    )
```

```python
import functools
import math
import jax
import jax.numpy as jnp
from jax import lax
from jax.experimental import pallas as pl
from jax.experimental.pallas import tpu as pltpu
from jax.sharding import PartitionSpec as P

SWEEPS = 2


def xor_pairs(size, mask):
    return [(i, i ^ mask) for i in range(size)]


def prepare_kernel(tile_rows, tile_cols, groups, masks_ref, code_ref, tiles_ref, where_ref, first_ref, sem):
    copies = start_copies(tiles_ref, 0, first_ref, sem)
    my_col = lax.axis_index("col")
    code = code_ref[...]
    live = code >= 0
    code = jnp.maximum(code, 0)
    col, row, coupling = split_code(code, tile_rows, tile_cols)
    mask = jnp.zeros_like(code)
    for i in range(masks_ref.shape[0]):
        mask = jnp.where(coupling == i + 1, masks_ref[i], mask)
    place = jnp.right_shift(mask, 1) + jnp.bitwise_and(mask, 1) * (groups // 2)
    row = jnp.bitwise_xor(row, my_col * tile_cols)
    where_ref[0] = jnp.where(live, place * tile_cols + col, 0)
    where_ref[1] = jnp.where(live, row, tile_rows)
    for copy in copies:
        copy.wait()


def split_code(code, tile_rows, tile_cols):
    def divide(a, n):
        if n & (n - 1):
            return a // n, a % n
        return jnp.right_shift(a, n.bit_length() - 1), jnp.bitwise_and(a, n - 1)

    rest, col = divide(code, tile_cols)
    coupling, row = divide(rest, tile_rows)
    return col, row, coupling


def start_copies(tiles_ref, start, out_ref, sem):
    chunks = sem.shape[0]
    size = out_ref.shape[0] // chunks
    copies = []
    for i in range(chunks):
        copies.append(
            pltpu.make_async_copy(
                tiles_ref.at[pl.ds(start + i * size, size)], out_ref.at[pl.ds(i * size, size)], sem.at[i]
            )
        )
        copies[-1].start()
    return copies


def prepare(xor_masks, tile_index, tiles, tile_rows, tile_cols, groups):
    slots, tile_size = tiles.shape[0], tiles.shape[1]
    lanes = math.gcd(slots, 128)
    first = slots // 2
    vmem = pl.BlockSpec(memory_space=pltpu.VMEM)
    where, first_tiles = pl.pallas_call(
        functools.partial(prepare_kernel, tile_rows, tile_cols, groups),
        out_shape=[
            jax.ShapeDtypeStruct((2, slots // lanes, lanes), jnp.int32),
            jax.ShapeDtypeStruct((first, tile_size, tile_size), tiles.dtype),
        ],
        in_specs=[pl.BlockSpec(memory_space=pltpu.SMEM), vmem, pl.BlockSpec(memory_space=pl.ANY)],
        out_specs=[vmem, vmem],
        scratch_shapes=[pltpu.SemaphoreType.DMA((math.gcd(first, 4),))],
        compiler_params=pltpu.CompilerParams(vmem_limit_bytes=(52 << 20) - tiles.size * 2),
        cost_estimate=pl.CostEstimate(flops=0, bytes_accessed=tiles.size * 2, transcendentals=0),
        name="prepare",
    )(xor_masks, tile_index.reshape(slots // lanes, lanes), tiles)
    return where.reshape(2, slots), first_tiles


def add_products(unroll, start, where_ref, source_ref, tiles_ref, acc):
    slots, tile_size = tiles_ref.shape[0], tiles_ref.shape[1]
    states = source_ref.shape[1]

    @pl.loop(0, slots // unroll)
    def _(step):
        products = []
        for pair in range(0, unroll, 2):
            slot = step * unroll + pair
            picked = jnp.concatenate([source_ref[where_ref[0, start + slot + i]] for i in range(2)], axis=0)
            two = tiles_ref[pl.ds(slot, 2)].reshape(2 * tile_size, tile_size)
            product = lax.dot_general(picked, two, (((1,), (1,)), ((), ())), preferred_element_type=jnp.float32)
            products += [product[:states, :tile_size], product[states:, tile_size:]]
        for i in range(unroll):
            acc[where_ref[1, start + step * unroll + i]] += products[i]


def product_kernel(quarters, unroll, copying, where_ref, source_ref, first_ref, second_ref, *refs):
    outs, acc = refs[:quarters], refs[-2] if copying else refs[-1]
    copies, first = [], first_ref.shape[0]
    if copying:
        copies = start_copies(second_ref, first, refs[quarters], refs[-1])
        second_ref = refs[quarters]
    acc[...] = jnp.zeros_like(acc)
    add_products(unroll, 0, where_ref, source_ref, first_ref, acc)
    for copy in copies:
        copy.wait()
    add_products(unroll, first, where_ref, source_ref, second_ref, acc)
    rows = outs[0].shape[0]
    for i, out in enumerate(outs):
        out[...] = acc[i * rows : (i + 1) * rows].astype(out.dtype)


def tile_products(where, source, first_tiles, second_tiles, quarters, rows):
    slots, tile_size = where.shape[1], first_tiles.shape[1]
    states, first = source.shape[1], first_tiles.shape[0]
    copying = second_tiles.shape[0] == slots
    block = (rows, states, tile_size)
    vmem = pl.BlockSpec(memory_space=pltpu.VMEM)
    shapes = [jax.ShapeDtypeStruct(block, jnp.float32 if i == 0 else jnp.bfloat16) for i in range(quarters)]
    scratch = [pltpu.VMEM((quarters * rows + 1, states, tile_size), jnp.float32)]
    if copying:
        shapes.append(jax.ShapeDtypeStruct((slots - first, tile_size, tile_size), first_tiles.dtype))
        scratch.append(pltpu.SemaphoreType.DMA((math.gcd(slots - first, 4),)))
    return pl.pallas_call(
        functools.partial(product_kernel, quarters, math.gcd(math.gcd(first, slots - first), 64), copying),
        out_shape=shapes,
        in_specs=[
            pl.BlockSpec(memory_space=pltpu.SMEM), vmem, vmem, pl.BlockSpec(memory_space=pl.ANY) if copying else vmem
        ],
        out_specs=[vmem] * len(shapes),
        scratch_shapes=scratch,
        compiler_params=pltpu.CompilerParams(vmem_limit_bytes=(52 << 20) - slots * tile_size * tile_size * 2),
        cost_estimate=pl.CostEstimate(
            flops=2 * slots * states * tile_size * tile_size, bytes_accessed=0, transcendentals=0
        ),
        name="tile_products",
    )(where, source, first_tiles, second_tiles)


def per_device(states, gaps, tiles, tile_index, xor_masks, ritz_level):
    groups, quarters = lax.axis_size("grp"), lax.axis_size("col")
    state_count, row_slice = states.shape
    tile_size = tiles.shape[1]
    tile_cols = row_slice // tile_size
    tile_rows = tile_cols * quarters

    def blocked(a):
        if a.ndim == 3:
            return a
        return jnp.transpose(a.reshape(state_count, tile_cols, tile_size), (1, 0, 2))

    where, first_tiles = prepare(xor_masks, tile_index, tiles, tile_rows, tile_cols, groups)
    second_tiles = tiles
    shifts = (ritz_level.astype(jnp.float32) * 0.125 - 1.0)[None, :, None]
    gaps = blocked(gaps)
    current = states
    for sweep in range(SWEEPS):
        near = [current] + [lax.ppermute(current, "grp", xor_pairs(groups, k)) for k in range(2, groups, 2)]
        near = jnp.concatenate([blocked(a) for a in near], axis=0)
        far = lax.ppermute(near, "grp", xor_pairs(groups, 1))
        source = jnp.concatenate([near, far], axis=0)
        sums = tile_products(where, source, first_tiles, second_tiles, quarters, tile_cols)
        if sweep == 0:
            second_tiles = sums[quarters]
        product_sum = sums[0]
        for k in range(1, quarters):
            product_sum = product_sum + lax.ppermute(sums[k], "col", xor_pairs(quarters, k)).astype(jnp.float32)
        previous = blocked(current).astype(jnp.float32)
        updated = previous - (product_sum - shifts * previous) / gaps
        current = updated.astype(jnp.bfloat16)
    return jnp.transpose(updated, (1, 0, 2)).reshape(state_count, row_slice)


def solution(mesh):
    placed = (
        P(None, ("grp", "col")),
        P(None, ("grp", "col")),
        P(("grp", "col"), None, None),
        P(("grp", "col")),
        P(),
        P(),
    )
    return jax.shard_map(
        per_device, mesh=mesh, in_specs=placed, out_specs=P(None, ("grp", "col")), check_vma=False
    )
```

```python
import functools
import math
import jax
import jax.numpy as jnp
from jax import lax
from jax.experimental import pallas as pl
from jax.experimental.pallas import tpu as pltpu
from jax.sharding import PartitionSpec as P

SWEEPS = 2
GRANT = 50 << 20


def xor_pairs(size, mask):
    return [(i, i ^ mask) for i in range(size)]


def divide(a, n):
    if n & (n - 1):
        return a // n, a % n
    return jnp.right_shift(a, n.bit_length() - 1), jnp.bitwise_and(a, n - 1)


def packing(groups, tile_rows, tile_cols):
    row_bits = tile_rows.bit_length()
    return row_bits, row_bits + (groups // 2 * tile_cols - 1).bit_length()


def prepare_kernel(groups, slots, mask_count, tile_rows, chunks, packed_ref, tiles_hbm, list_ref, current_ref, tiles_ref, sem):
    size = tiles_hbm.shape[0] // sem.shape[0]
    copies = [
        pltpu.make_async_copy(tiles_hbm.at[pl.ds(i * size, size)], tiles_ref.at[pl.ds(i * size, size)], sem.at[i])
        for i in range(sem.shape[0])
    ]
    for copy in copies:
        copy.start()

    tile_cols, states, tile_size = current_ref.shape
    for i in range(tile_cols):
        current_ref[i] = packed_ref[:states, i * tile_size : (i + 1) * tile_size].astype(current_ref.dtype)

    lanes = list_ref.shape[1]
    lines = slots // lanes
    code = [packed_ref[states : states + 1, i * lanes : (i + 1) * lanes] for i in range(lines)]
    code = jnp.concatenate(code, axis=0).astype(jnp.int32)
    source_at, slot_at = packing(groups, tile_rows, tile_cols)
    live = code >= 0
    rest, col = divide(jnp.maximum(code, 0), tile_cols)
    coupling, row = divide(rest, tile_rows)
    mask = jnp.zeros_like(code)
    for i in range(mask_count):
        value = jnp.broadcast_to(packed_ref[states + 1 : states + 2, i : i + 1], mask.shape).astype(jnp.int32)
        mask = jnp.where(coupling == i + 1, value, mask)
    kind = jnp.where(mask == 0, 0, 1 + jnp.bitwise_and(mask, 1))
    kind = jnp.where(live, kind, 3)
    row = jnp.bitwise_xor(row, lax.axis_index("col") * tile_cols)
    source = jnp.right_shift(mask, 1) * tile_cols + col
    entry = row + jnp.left_shift(source, source_at)

    def column(a):
        parts = [jnp.broadcast_to(a[i : i + 1].astype(jnp.float32), (lanes, lanes)).T for i in range(lines)]
        return jnp.concatenate(parts, axis=0).astype(jnp.int32)

    kind_col, entry_col = column(kind), column(entry)
    slot_col = lax.broadcasted_iota(jnp.int32, (slots, lanes), 0)
    lane = lax.broadcasted_iota(jnp.int32, (slots, lanes), 1)
    entry_col = entry_col + jnp.left_shift(slot_col, slot_at)
    earlier = jnp.zeros((slots, lanes), jnp.int32)
    for i in range(lines):
        same = jnp.broadcast_to(kind[i : i + 1], (slots, lanes)) == kind_col
        earlier += jnp.where(same & (lane + i * lanes < slot_col), 1, 0)
    place = jnp.sum(earlier, axis=1, keepdims=True)
    start = jnp.int32(0)
    shift = jnp.zeros((slots, lanes), jnp.int32)
    info = jnp.zeros((1, lanes), jnp.int32)
    info_lane = lax.broadcasted_iota(jnp.int32, (1, lanes), 1)
    for k in range(3):
        shift = jnp.where(kind_col == k, start, shift)
        steps = (jnp.sum(jnp.where(kind == k, 1, 0)) + chunks - 1) // chunks
        info = jnp.where(info_lane == k, start // chunks, info)
        start = start + steps * chunks
    info = jnp.where(info_lane == 3, start // chunks, info)
    place = jnp.where(kind_col == 3, -1, place + shift)
    for i in range(list_ref.shape[0] - 1):
        hit = place == lane + i * lanes
        found = jnp.sum(jnp.where(hit, entry_col - tile_rows, 0), axis=0, keepdims=True)
        list_ref[i : i + 1] = found + tile_rows
    list_ref[list_ref.shape[0] - 1 :] = info
    for copy in copies:
        copy.wait()


def prepare(xor_masks, tile_index, states, tiles, tile_rows, groups, chunks):
    slots, tile_size = tiles.shape[0], tiles.shape[1]
    state_count, row_slice = states.shape
    lanes = math.gcd(slots, 128)
    lines = -(-(slots + 3 * chunks) // lanes) + 1
    vmem = pl.BlockSpec(memory_space=pltpu.VMEM)
    packed = [states, tile_index[None], xor_masks[None]]
    packed = [a.astype(jnp.float32) for a in packed]
    packed = jnp.concatenate([jnp.pad(a, ((0, 0), (0, row_slice - a.shape[1]))) for a in packed], axis=0)
    return pl.pallas_call(
        functools.partial(prepare_kernel, groups, slots, xor_masks.shape[0], tile_rows, chunks),
        out_shape=[
            jax.ShapeDtypeStruct((lines, lanes), jnp.int32),
            jax.ShapeDtypeStruct((row_slice // tile_size, state_count, tile_size), states.dtype),
            jax.ShapeDtypeStruct(tiles.shape, tiles.dtype),
        ],
        in_specs=[vmem, pl.BlockSpec(memory_space=pl.ANY)],
        out_specs=[vmem] * 3,
        scratch_shapes=[pltpu.SemaphoreType.DMA((math.gcd(slots, 8),))],
        compiler_params=pltpu.CompilerParams(vmem_limit_bytes=GRANT - tiles.size * 2),
        cost_estimate=pl.CostEstimate(flops=0, bytes_accessed=tiles.size * 2, transcendentals=0),
        name="prepare",
    )(packed, tiles)


def product_kernel(kind, chunks, source_at, slot_at, list_ref, source_ref, tiles_ref, *refs):
    lines, lanes = list_ref.shape
    tile_size, states = tiles_ref.shape[1], source_ref.shape[1]
    if kind == 0:
        acc = refs[0]
        acc[...] = jnp.zeros_like(acc)
    elif kind == 1:
        acc = refs[1]
        acc[...] = refs[0][...]
    else:
        acc, outs = refs[-1], refs[1:-1]
        acc[...] = refs[0][...]

    @pl.loop(list_ref[lines - 1, kind], list_ref[lines - 1, kind + 1])
    def _(step):
        line, lane = divide(step * chunks, lanes)
        entries = [list_ref[line, lane + i] for i in range(chunks)]
        products = []
        for pair in range(0, chunks, 2):
            picked, two = [], []
            for i in range(2):
                entry = entries[pair + i]
                source = jnp.bitwise_and(jnp.right_shift(entry, source_at), (1 << (slot_at - source_at)) - 1)
                picked.append(source_ref[source])
                two.append(tiles_ref[jnp.right_shift(entry, slot_at)])
            product = lax.dot_general(
                jnp.concatenate(picked, axis=0),
                jnp.concatenate(two, axis=0),
                (((1,), (1,)), ((), ())),
                preferred_element_type=jnp.float32,
            )
            products += [product[:states, :tile_size], product[states:, tile_size:]]
        for i in range(chunks):
            acc[jnp.bitwise_and(entries[i], (1 << source_at) - 1)] += products[i]

    if kind == 2:
        rows = outs[0].shape[0]
        for i, out in enumerate(outs):
            out[...] = acc[i * rows : (i + 1) * rows].astype(out.dtype)


def tile_products(kind, slot_list, source, tiles, sums, quarters, rows, groups, chunks):
    slots, tile_size = tiles.shape[0], tiles.shape[1]
    states = source.shape[1]
    whole = jax.ShapeDtypeStruct((quarters * rows + 1, states, tile_size), jnp.float32)
    source_at, slot_at = packing(groups, quarters * rows, rows)
    vmem = pl.BlockSpec(memory_space=pltpu.VMEM)
    operands, shapes, scratch, aliases = [slot_list, source, tiles], whole, [], {}
    if kind > 0:
        operands.append(sums)
    if kind == 2:
        shapes = [
            jax.ShapeDtypeStruct((rows, states, tile_size), jnp.float32 if i == 0 else jnp.bfloat16)
            for i in range(quarters)
        ]
        scratch = [pltpu.VMEM(whole.shape, whole.dtype)]
    return pl.pallas_call(
        functools.partial(product_kernel, kind, chunks, source_at, slot_at),
        out_shape=shapes,
        in_specs=[pl.BlockSpec(memory_space=pltpu.SMEM)] + [vmem] * (len(operands) - 1),
        out_specs=[vmem] * quarters if kind == 2 else vmem,
        scratch_shapes=scratch,
        input_output_aliases=aliases,
        compiler_params=pltpu.CompilerParams(vmem_limit_bytes=16 << 20),
        cost_estimate=pl.CostEstimate(
            flops=slots * states * tile_size * tile_size, bytes_accessed=0, transcendentals=0
        ),
        name=("own_products", "even_products", "odd_products")[kind],
    )(*operands)


def per_device(states, gaps, tiles, tile_index, xor_masks, ritz_level):
    groups, quarters = lax.axis_size("grp"), lax.axis_size("col")
    state_count, row_slice = states.shape
    tile_size = tiles.shape[1]
    tile_cols = row_slice // tile_size
    tile_rows = tile_cols * quarters
    chunks = 32

    def blocked(a):
        if a.ndim == 3:
            return a
        return jnp.transpose(a.reshape(state_count, tile_cols, tile_size), (1, 0, 2))

    slot_list, current, tiles = prepare(xor_masks, tile_index, states, tiles, tile_rows, groups, chunks)
    shifts = (ritz_level.astype(jnp.float32) * 0.125 - 1.0)[None, :, None]
    gaps = blocked(gaps)
    sizes = (quarters, tile_cols, groups, chunks)
    for sweep in range(SWEEPS):
        sent = states if sweep == 0 else current
        near = [lax.ppermute(sent, "grp", xor_pairs(groups, k)) for k in range(2, groups, 2)]
        sums = tile_products(0, slot_list, current, tiles, None, *sizes)
        near, sums = lax.optimization_barrier((near, sums))
        near = jnp.concatenate([current] + [blocked(a) for a in near], axis=0)
        far = lax.ppermute(near, "grp", xor_pairs(groups, 1))
        sums = tile_products(1, slot_list, near, tiles, sums, *sizes)
        sums = tile_products(2, slot_list, far, tiles, sums, *sizes)
        product_sum = sums[0]
        for k in range(1, quarters):
            product_sum = product_sum + lax.ppermute(sums[k], "col", xor_pairs(quarters, k)).astype(jnp.float32)
        previous = current.astype(jnp.float32)
        updated = previous - (product_sum - shifts * previous) / gaps
        current = updated.astype(jnp.bfloat16)
    return jnp.transpose(updated, (1, 0, 2)).reshape(state_count, row_slice)


def solution(mesh):
    placed = (
        P(None, ("grp", "col")),
        P(None, ("grp", "col")),
        P(("grp", "col"), None, None),
        P(("grp", "col")),
        P(),
        P(),
    )
    return jax.shard_map(
        per_device, mesh=mesh, in_specs=placed, out_specs=P(None, ("grp", "col")), check_vma=False
    )
```

```python
import functools
import math
import jax
import jax.numpy as jnp
from jax import lax
from jax.experimental import pallas as pl
from jax.experimental.pallas import tpu as pltpu
from jax.sharding import PartitionSpec as P

SWEEPS = 2
GRANT = 50 << 20


def xor_pairs(size, mask):
    return [(i, i ^ mask) for i in range(size)]


def first_step_kernel(out_ref):
    out_ref[...] = jnp.zeros_like(out_ref)


def first_step(tiles):
    return pl.pallas_call(
        first_step_kernel,
        out_shape=jax.ShapeDtypeStruct((8, 128), jnp.float32),
        out_specs=pl.BlockSpec(memory_space=pltpu.VMEM),
        compiler_params=pltpu.CompilerParams(vmem_limit_bytes=1 << 20),
        cost_estimate=pl.CostEstimate(flops=4 * 10**9, bytes_accessed=0, transcendentals=0),
        name="first_step",
    )()


def divide(a, n):
    if n & (n - 1):
        return a // n, a % n
    return jnp.right_shift(a, n.bit_length() - 1), jnp.bitwise_and(a, n - 1)


def packing(groups, tile_rows, tile_cols):
    row_bits = tile_rows.bit_length()
    return row_bits, row_bits + (groups // 2 * tile_cols - 1).bit_length()


def prepare_kernel(groups, slots, mask_count, tile_rows, chunks, packed_ref, tick_ref, slots_ref, current_ref, list_ref, list_sem):
    copies = []
    tile_cols, states, tile_size = current_ref.shape
    for i in range(tile_cols):
        current_ref[i] = packed_ref[:states, i * tile_size : (i + 1) * tile_size].astype(current_ref.dtype)

    lanes = list_ref.shape[1]
    lines = slots // lanes
    code = [packed_ref[states : states + 1, i * lanes : (i + 1) * lanes] for i in range(lines)]
    code = jnp.concatenate(code, axis=0).astype(jnp.int32)
    source_at, slot_at = packing(groups, tile_rows, tile_cols)
    live = code >= 0
    rest, col = divide(jnp.maximum(code, 0), tile_cols)
    coupling, row = divide(rest, tile_rows)
    mask = jnp.zeros_like(code)
    for i in range(mask_count):
        value = jnp.broadcast_to(packed_ref[states + 1 : states + 2, i : i + 1], mask.shape).astype(jnp.int32)
        mask = jnp.where(coupling == i + 1, value, mask)
    kind = jnp.where(mask == 0, 0, 1 + jnp.bitwise_and(mask, 1))
    kind = jnp.where(live, kind, 3)
    row = jnp.bitwise_xor(row, lax.axis_index("col") * tile_cols)
    source = jnp.right_shift(mask, 1) * tile_cols + col
    entry = row + jnp.left_shift(source, source_at)

    def column(a):
        parts = [jnp.broadcast_to(a[i : i + 1].astype(jnp.float32), (lanes, lanes)).T for i in range(lines)]
        return jnp.concatenate(parts, axis=0).astype(jnp.int32)

    kind_col, entry_col = column(kind), column(entry)
    slot_col = lax.broadcasted_iota(jnp.int32, (slots, lanes), 0)
    lane = lax.broadcasted_iota(jnp.int32, (slots, lanes), 1)
    entry_col = entry_col + jnp.left_shift(slot_col, slot_at)
    earlier = jnp.zeros((slots, lanes), jnp.int32)
    for i in range(lines):
        same = jnp.broadcast_to(kind[i : i + 1], (slots, lanes)) == kind_col
        earlier += jnp.where(same & (lane + i * lanes < slot_col), 1, 0)
    place = jnp.sum(earlier, axis=1, keepdims=True)
    start = jnp.int32(0)
    shift = jnp.zeros((slots, lanes), jnp.int32)
    info = jnp.zeros((1, lanes), jnp.int32)
    info_lane = lax.broadcasted_iota(jnp.int32, (1, lanes), 1)
    for k in range(3):
        shift = jnp.where(kind_col == k, start, shift)
        steps = (jnp.sum(jnp.where(kind == k, 1, 0)) + chunks - 1) // chunks
        info = jnp.where(info_lane == k, start // chunks, info)
        start = start + steps * chunks
    info = jnp.where(info_lane == 3, start // chunks, info)
    place = jnp.where(kind_col == 3, -1, place + shift)
    for i in range(list_ref.shape[0] - 1):
        hit = place == lane + i * lanes
        found = jnp.sum(jnp.where(hit, entry_col - tile_rows, 0), axis=0, keepdims=True)
        list_ref[i : i + 1] = found + tile_rows
    list_ref[list_ref.shape[0] - 1 :] = info
    copies.append(pltpu.make_async_copy(list_ref, slots_ref, list_sem))
    copies[-1].start()
    for copy in copies:
        copy.wait()


def prepare(xor_masks, tile_index, states, tiles, tile_rows, groups, chunks):
    slots, tile_size = tiles.shape[0], tiles.shape[1]
    state_count, row_slice = states.shape
    lanes = math.gcd(slots, 128)
    lines = -(-(slots + 3 * chunks) // lanes) + 1
    vmem = pl.BlockSpec(memory_space=pltpu.VMEM)
    tick = first_step(tiles)
    states, tile_index, xor_masks, tick = lax.optimization_barrier((states, tile_index, xor_masks, tick))
    packed = [states, tile_index[None], xor_masks[None]]
    packed = [a.astype(jnp.float32) for a in packed]
    packed = jnp.concatenate([jnp.pad(a, ((0, 0), (0, row_slice - a.shape[1]))) for a in packed], axis=0)
    return pl.pallas_call(
        functools.partial(prepare_kernel, groups, slots, xor_masks.shape[0], tile_rows, chunks),
        out_shape=[
            pltpu.SMEM((lines, lanes), jnp.int32),
            jax.ShapeDtypeStruct((row_slice // tile_size, state_count, tile_size), states.dtype),
        ],
        in_specs=[vmem, vmem],
        out_specs=[pl.BlockSpec(memory_space=pltpu.SMEM), vmem],
        scratch_shapes=[
            pltpu.VMEM((lines, lanes), jnp.int32),
            pltpu.SemaphoreType.DMA,
        ],
        compiler_params=pltpu.CompilerParams(vmem_limit_bytes=GRANT - tiles.size * 2),
        cost_estimate=pl.CostEstimate(flops=4 * 10**9, bytes_accessed=0, transcendentals=0),
        name="prepare",
    )(packed, tick)


def product_kernel(kind, chunks, source_at, slot_at, list_ref, source_ref, tiles_ref, *refs):
    lines, lanes = list_ref.shape
    tile_size, states = tiles_ref.shape[1], source_ref.shape[1]
    if kind == 0:
        acc = refs[0]
        acc[...] = jnp.zeros_like(acc)
    elif kind == 1:
        acc = refs[1]
        acc[...] = refs[0][...]
    else:
        acc, outs = refs[-1], refs[1:-1]
        acc[...] = refs[0][...]

    @pl.loop(list_ref[lines - 1, kind], list_ref[lines - 1, kind + 1])
    def _(step):
        line, lane = divide(step * chunks, lanes)
        entries = [list_ref[line, lane + i] for i in range(chunks)]
        products = []
        for pair in range(0, chunks, 2):
            picked, two = [], []
            for i in range(2):
                entry = entries[pair + i]
                source = jnp.bitwise_and(jnp.right_shift(entry, source_at), (1 << (slot_at - source_at)) - 1)
                picked.append(source_ref[source])
                two.append(tiles_ref[jnp.right_shift(entry, slot_at)])
            product = lax.dot_general(
                jnp.concatenate(picked, axis=0),
                jnp.concatenate(two, axis=0),
                (((1,), (1,)), ((), ())),
                preferred_element_type=jnp.float32,
            )
            products += [product[:states, :tile_size], product[states:, tile_size:]]
        for i in range(chunks):
            acc[jnp.bitwise_and(entries[i], (1 << source_at) - 1)] += products[i]

    if kind == 2:
        rows = outs[0].shape[0]
        for i, out in enumerate(outs):
            out[...] = acc[i * rows : (i + 1) * rows].astype(out.dtype)


def tile_products(kind, slot_list, source, tiles, sums, quarters, rows, groups, chunks):
    slots, tile_size = tiles.shape[0], tiles.shape[1]
    states = source.shape[1]
    whole = jax.ShapeDtypeStruct((quarters * rows + 1, states, tile_size), jnp.float32)
    source_at, slot_at = packing(groups, quarters * rows, rows)
    vmem = pl.BlockSpec(memory_space=pltpu.VMEM)
    operands, shapes, scratch, aliases = [slot_list, source, tiles], whole, [], {}
    if kind > 0:
        operands.append(sums)
    if kind == 2:
        shapes = [
            jax.ShapeDtypeStruct((rows, states, tile_size), jnp.float32 if i == 0 else jnp.bfloat16)
            for i in range(quarters)
        ]
        scratch = [pltpu.VMEM(whole.shape, whole.dtype)]
    return pl.pallas_call(
        functools.partial(product_kernel, kind, chunks, source_at, slot_at),
        out_shape=shapes,
        in_specs=[pl.BlockSpec(memory_space=pltpu.SMEM)] + [vmem] * (len(operands) - 1),
        out_specs=[vmem] * quarters if kind == 2 else vmem,
        scratch_shapes=scratch,
        input_output_aliases=aliases,
        compiler_params=pltpu.CompilerParams(vmem_limit_bytes=16 << 20),
        cost_estimate=pl.CostEstimate(
            flops=slots * states * tile_size * tile_size, bytes_accessed=0, transcendentals=0
        ),
        name=("own_products", "even_products", "odd_products")[kind],
    )(*operands)


def per_device(states, gaps, tiles, tile_index, xor_masks, ritz_level):
    groups, quarters = lax.axis_size("grp"), lax.axis_size("col")
    state_count, row_slice = states.shape
    tile_size = tiles.shape[1]
    tile_cols = row_slice // tile_size
    tile_rows = tile_cols * quarters
    chunks = 32

    def blocked(a):
        if a.ndim == 3:
            return a
        return jnp.transpose(a.reshape(state_count, tile_cols, tile_size), (1, 0, 2))

    slot_list, current = prepare(xor_masks, tile_index, states, tiles, tile_rows, groups, chunks)
    shifts = (ritz_level.astype(jnp.float32) * 0.125 - 1.0)[None, :, None]
    gaps = blocked(gaps)
    sizes = (quarters, tile_cols, groups, chunks)
    for sweep in range(SWEEPS):
        sent = states if sweep == 0 else current
        near = [lax.ppermute(sent, "grp", xor_pairs(groups, k)) for k in range(2, groups, 2)]
        sums = tile_products(0, slot_list, current, tiles, None, *sizes)
        if sweep > 0:
            near, sums = lax.optimization_barrier((near, sums))
        near = jnp.concatenate([current] + [blocked(a) for a in near], axis=0)
        far = lax.ppermute(near, "grp", xor_pairs(groups, 1))
        sums = tile_products(1, slot_list, near, tiles, sums, *sizes)
        sums = tile_products(2, slot_list, far, tiles, sums, *sizes)
        product_sum = sums[0]
        for k in range(1, quarters):
            product_sum = product_sum + lax.ppermute(sums[k], "col", xor_pairs(quarters, k)).astype(jnp.float32)
        previous = current.astype(jnp.float32)
        updated = previous - (product_sum - shifts * previous) / gaps
        current = updated.astype(jnp.bfloat16)
    return jnp.transpose(updated, (1, 0, 2)).reshape(state_count, row_slice)


def solution(mesh):
    placed = (
        P(None, ("grp", "col")),
        P(None, ("grp", "col")),
        P(("grp", "col"), None, None),
        P(("grp", "col")),
        P(),
        P(),
    )
    return jax.shard_map(
        per_device, mesh=mesh, in_specs=placed, out_specs=P(None, ("grp", "col")), check_vma=False
    )
```
